768 devices in a mesh: seq: 64 (over y, x, core), head: 12 (over z).
Axes of the slice: x: 4, y: 8, z: 12, core: 2. Of those that a mesh axis runs over, the one named last changes fastest.
Arguments:
- query_rows: bfloat16 [32768, 6144], P('seq', 'head'), may hold values from -6 to 6
- key_rows: bfloat16 [32768, 384], P('seq'), may hold values from -6 to 6
- value_rows: bfloat16 [32768, 384], P('seq'), may hold values from -6 to 6
- output_grad: bfloat16 [32768, 6144], P('seq', 'head'), may hold values from -0.59765625 to 0.59765625
- log_norm: float32 [48, 32768], P('head', 'seq'), may hold values from 0.5 to 3
- row_delta: float32 [48, 32768], P('head', 'seq'), may hold values from -5 to 5
- dispatch: int32 [64, 64], replicated, may hold values from 0 to 63, as said below
- listed_spans: int32 [64, 16], replicated, may hold values from 0 to 1023, as said below
- range_start: int32 [64, 64], replicated, may hold values from 0 to 32760, as said below
Outputs:
- query_grad: bfloat16 [32768, 6144], P('seq', 'head')
- key_grad: float32 [384, 32768], P('head', 'seq')
- value_grad: float32 [384, 32768], P('head', 'seq')
The draws below stay inside these ranges and needn't reach their ends.
Inputs may be any that keep to these rules, and one draw needn't show every extreme that they name: `dispatch`: entry [h, j] names the group of query span 64 * h + j. Every group holds exactly 64 spans, and each row gives at most 1 spans to any one group, a number that every row reaches. `listed_spans`: row g holds 16 distinct key spans for group g. At most 1 of them lie among the 16 key spans of one index of seq, and every row reaches that number. `range_start`: entry [h, j] is at most 8 * (64 * h + j).
All inputs are finite; a program needn't handle non-finite values.
Results may differ from the reference program's by a relative error of at most 0.0046.
Values may be sent and summed in bfloat16 or wider, within the bound.
No kernel may reach another device: no remote copies, remote signals or barrier semaphores. Data moves between devices by JAX's collectives and lax.ppermute only.
A program may use at most 32 MiB of HBM per device.

```python
import math
import jax
import jax.numpy as jnp
from jax import lax

HD = 128
GROUP = 16
SPAN = 8
KVCH = 32
NLIST = 16
CH_DEV = 64
HQ = 48
KVH = 3
OWNERS = 64
KV_DEV = 16
TOKENS = 32768


def draw_dispatch(key, part):
    first, second, third = jax.random.split(jax.random.fold_in(key, 11), 3)
    groups = min(OWNERS, CH_DEV)
    shuffle = jax.random.permutation(first, OWNERS)
    offsets = jax.random.permutation(second, OWNERS)[:groups]
    rotate = jax.random.randint(third, (OWNERS,), 0, CH_DEV)
    homes = jnp.arange(OWNERS, dtype=jnp.int32)[:, None]
    picks = (jnp.arange(CH_DEV, dtype=jnp.int32)[None, :] + rotate[:, None]) % CH_DEV % groups
    return shuffle[(homes + offsets[picks]) % OWNERS].astype(jnp.int32)


def draw_listed_spans(key, part):
    first, second, third = jax.random.split(jax.random.fold_in(key, 23), 3)
    groups = min(OWNERS, NLIST)
    per_home = NLIST // groups
    homes = jax.vmap(lambda item: jax.random.permutation(item, OWNERS)[:groups])(jax.random.split(first, OWNERS))
    subs = jax.vmap(lambda item: jax.random.permutation(item, KV_DEV)[:per_home])(jax.random.split(second, OWNERS * groups))
    chosen = (homes[:, :, None] * KV_DEV + subs.reshape(OWNERS, groups, per_home)).reshape(OWNERS, NLIST)
    shuffles = jax.vmap(lambda item: jax.random.permutation(item, NLIST))(jax.random.split(third, OWNERS))
    return jnp.take_along_axis(chosen, shuffles, axis=1).astype(jnp.int32)


def draw_range_start(key, part):
    span_ids = jnp.arange(OWNERS * CH_DEV, dtype=jnp.int32).reshape(OWNERS, CH_DEV)
    reach = jax.random.randint(jax.random.fold_in(key, 37), (OWNERS, CH_DEV), SPAN, TOKENS + 1)
    return jnp.maximum(0, (span_ids + 1) * SPAN - reach).astype(jnp.int32)


def steps_of(stream_key, dims, cuts, low, top_value):
    loudness = 1.0
    for dim, shards_of in cuts:
        heights = jax.random.uniform(jax.random.fold_in(jax.random.fold_in(stream_key, 6), dim), (shards_of,), jnp.float32, low / len(cuts), top_value / len(cuts))
        loudness = loudness * jnp.repeat(jnp.exp(heights), dims[dim] // shards_of).reshape((-1,) + (1,) * (len(dims) - 1 - dim))
    return loudness


def noise(rng, dims, spread, most, pieces=(), held_as=jnp.bfloat16):
    entries = jax.random.normal(rng, dims, jnp.float32) * spread
    if len(pieces) > 0:
        entries = steps_of(rng, dims, pieces, -0.22, 0.18) * entries
    return jnp.clip(entries, min=-most, max=most).astype(held_as)


def setup_inputs(seed: int = 0) -> dict:
    seeds = jax.random.split(jax.random.key(seed), 10)
    return {
        "query_rows": noise(seeds[0], (TOKENS, HQ * HD), 1.0, 6.0, ((0, 64), (1, 12))),
        "key_rows": noise(seeds[1], (TOKENS, KVH * HD), 1.0, 6.0, ((0, 64),)),
        "value_rows": noise(seeds[2], (TOKENS, KVH * HD), 1.0, 6.0, ((0, 64),)),
        "output_grad": noise(seeds[3], (TOKENS, HQ * HD), 0.09, 0.59765625, ((0, 64), (1, 12))),
        "log_norm": jnp.clip(0.5 + 2.5 * jax.random.uniform(seeds[4], (HQ, TOKENS), jnp.float32) ** steps_of(seeds[4], (HQ, TOKENS), ((0, 12), (1, 64)), -0.2, 0.2), 0.5, 3.0),
        "row_delta": noise(seeds[5], (HQ, TOKENS), 1.0, 5.0, ((0, 12), (1, 64)), jnp.float32),
        "dispatch": draw_dispatch(jax.random.fold_in(seeds[9], 71), 0),
        "listed_spans": draw_listed_spans(jax.random.fold_in(seeds[9], 71), 0),
        "range_start": draw_range_start(jax.random.fold_in(seeds[9], 71), 0),
    }


def reference(query_rows, key_rows, value_rows, output_grad, log_norm, row_delta, dispatch, listed_spans, range_start):
    owners = dispatch.shape[0]
    spans = dispatch.shape[1]
    score_scale = 1.0 / math.sqrt(HD)
    order = jnp.argsort(dispatch.reshape(-1), stable=True).astype(jnp.int32).reshape(owners, spans)
    starts = range_start.reshape(-1)
    query_all = query_rows.reshape(TOKENS, KVH, GROUP, HD)
    grad_all = output_grad.reshape(TOKENS, KVH, GROUP, HD)
    key_all = key_rows.reshape(TOKENS, KVH, HD)
    value_all = value_rows.reshape(TOKENS, KVH, HD)
    norm_all = log_norm.reshape(KVH, GROUP, TOKENS)
    delta_all = row_delta.reshape(KVH, GROUP, TOKENS)
    span_offsets = jnp.arange(SPAN, dtype=jnp.int32)
    block_offsets = jnp.arange(KVCH, dtype=jnp.int32)

    def one_owner(carry, owner):
        key_acc, value_acc = carry
        query_ids = order[owner]
        query_pos = (query_ids[:, None] * SPAN + span_offsets[None, :]).reshape(-1)
        key_pos = (listed_spans[owner][:, None] * KVCH + block_offsets[None, :]).reshape(-1)
        lowest = jnp.repeat(starts[query_ids], SPAN)
        allowed = (key_pos[None, :] <= query_pos[:, None]) & (key_pos[None, :] >= lowest[:, None])
        q_part = query_all[query_pos].astype(jnp.float32)
        g_part = grad_all[query_pos].astype(jnp.float32)
        k_part = key_all[key_pos].astype(jnp.float32)
        v_part = value_all[key_pos].astype(jnp.float32)
        scores = jnp.einsum('qagd,kad->agqk', q_part, k_part) * score_scale
        norms = norm_all[:, :, query_pos]
        deltas = delta_all[:, :, query_pos]
        probs = jnp.where(allowed[None, None], jnp.exp(scores - norms[..., None]), jnp.float32(0.0))
        dprobs = jnp.einsum('qagd,kad->agqk', g_part, v_part)
        dscores = probs * (dprobs - deltas[..., None])
        probs_round = lax.optimization_barrier(probs.astype(jnp.bfloat16)).astype(jnp.float32)
        dscores_round = lax.optimization_barrier(dscores.astype(jnp.bfloat16)).astype(jnp.float32)
        value_part = jnp.einsum('agqk,qagd->kad', probs_round, g_part)
        key_part = jnp.einsum('agqk,qagd->kad', dscores_round, q_part) * score_scale
        query_part = jnp.einsum('agqk,kad->qagd', dscores_round, k_part) * score_scale
        key_acc = key_acc.at[key_pos].add(key_part.reshape(-1, KVH * HD))
        value_acc = value_acc.at[key_pos].add(value_part.reshape(-1, KVH * HD))
        return ((key_acc, value_acc), query_part.reshape(-1, HQ * HD).astype(jnp.bfloat16))
    start_acc = (jnp.zeros((TOKENS, KVH * HD), jnp.float32), jnp.zeros((TOKENS, KVH * HD), jnp.float32))
    (key_acc, value_acc), stacked = lax.scan(one_owner, start_acc, jnp.arange(owners, dtype=jnp.int32))
    all_pos = (order.reshape(-1)[:, None] * SPAN + span_offsets[None, :]).reshape(-1)
    query_grad = jnp.zeros((TOKENS, HQ * HD), jnp.bfloat16).at[all_pos].set(stacked.reshape(-1, HQ * HD))
    return (query_grad, key_acc.T, value_acc.T)
```

```python
import math

import jax
import jax.numpy as jnp
from jax import lax
from jax.experimental import pallas as pl
from jax.experimental.pallas import tpu as pltpu
from jax.sharding import Mesh
from jax.sharding import PartitionSpec as P

HD = 128
GROUP = 16
SPAN = 8
KVCH = 32
NLIST = 16
SEQ = 64
MEM = 4
HEADS = 4
TOK = 512
QROWS = HEADS * SPAN
STAT = 2 * QROWS
KVROW = STAT + SPAN
IN_ROWS = KVROW + 16
OUT_ROWS = QROWS + 16
QUART = HD // MEM
SCALE = 1.0 / math.sqrt(HD)
LOG2E = math.log2(math.e)
BF = jnp.bfloat16
F32 = jnp.float32


def lane_select(member):
    depth = lax.broadcasted_iota(jnp.int32, (HD, HD), 0)
    lane = lax.broadcasted_iota(jnp.int32, (HD, HD), 1) % 64
    key_hot = (depth == QUART * member + lane) & (lane < QUART)
    value_hot = (depth == QUART * member + lane - QUART) & (lane >= QUART)
    return key_hot.astype(F32).astype(BF), value_hot.astype(F32).astype(BF)


def pack_kernel(dest, sub, place, q_ref, g_ref, k_ref, v_ref, norm_ref, delta_ref, out_ref, stat, rows, kv):
    key_hot, value_hot = lane_select(place[1])
    both = jnp.dot(k_ref[...], key_hot, preferred_element_type=F32) + jnp.dot(
        v_ref[...], value_hot, preferred_element_type=F32
    )
    both = both.reshape(NLIST, 2, 16, HD)
    lane = lax.broadcasted_iota(jnp.int32, (NLIST, 16, HD), 2)
    kv[...] = jnp.where(lane < 64, both[:, 0], both[:, 1]).astype(BF)
    stat[...] = jnp.zeros_like(stat)
    for index, ref in enumerate((norm_ref, delta_ref)):
        value = ref[...]
        top = value.astype(BF).astype(F32)
        stat[8 * index : 8 * index + 4, :] = top
        stat[8 * index + 4 : 8 * index + 8, :] = value - top
    rows[...] = stat[...].T.astype(BF).reshape(SEQ, SPAN, HD)

    for j in range(SEQ):
        slot = dest[j]
        for h in range(HEADS):
            at = pl.ds(SPAN * h, SPAN)
            out_ref[slot, at, :] = q_ref[j, :, HD * h : HD * h + HD]
            at = pl.ds(QROWS + SPAN * h, SPAN)
            out_ref[slot, at, :] = g_ref[j, :, HD * h : HD * h + HD]
        out_ref[slot, pl.ds(STAT, SPAN), :] = rows[j]
        out_ref[j, pl.ds(KVROW, 16), :] = kv[sub[j]]


def vmem():
    return pl.BlockSpec(memory_space=pltpu.VMEM)


def smem():
    return pl.BlockSpec(memory_space=pltpu.SMEM)


def pack(dest, sub, place, q, g, k, v, norm, delta):
    head_block = pl.BlockSpec((TOK, HD), lambda i, d, s, p: (0, p[0]))
    whole = lambda shape: pl.BlockSpec(shape, lambda i, d, s, p: (0,) * len(shape))
    return pl.pallas_call(
        pack_kernel,
        out_shape=jax.ShapeDtypeStruct((SEQ, IN_ROWS, HD), BF),
        grid_spec=pltpu.PrefetchScalarGridSpec(
            num_scalar_prefetch=3,
            grid=(1,),
            in_specs=[
                whole((SEQ, SPAN, HEADS * HD)),
                whole((SEQ, SPAN, HEADS * HD)),
                head_block,
                head_block,
                whole((HEADS, TOK)),
                whole((HEADS, TOK)),
            ],
            out_specs=whole((SEQ, IN_ROWS, HD)),
            scratch_shapes=[
                pltpu.VMEM((HD, TOK), F32),
                pltpu.VMEM((SEQ, SPAN, HD), BF),
                pltpu.VMEM((NLIST, 16, HD), BF),
            ],
        ),
        name="pack",
    )(dest, sub, place, q.reshape(SEQ, SPAN, -1), g.reshape(SEQ, SPAN, -1), k, v, norm, delta)


def select_kernel(homes, got_ref, out_ref):
    for i in range(NLIST):
        block = got_ref[homes[i], pl.ds(KVROW, 16), :]
        for m in range(MEM):
            out_ref[m, i] = block


def select(homes, got):
    return pl.pallas_call(
        select_kernel,
        out_shape=jax.ShapeDtypeStruct((MEM, NLIST, 16, HD), BF),
        in_specs=[smem(), vmem()],
        out_specs=vmem(),
        name="select",
    )(homes, got)


def attend_kernel(got_ref, kv_ref, bias_ref, dq_ref, dkv_ref, key, value, stat):
    for half in range(2):
        total = jnp.zeros((NLIST * 16, 2 * HD), F32)
        lane = lax.broadcasted_iota(jnp.int32, (HD, 2 * HD), 0)
        col = lax.broadcasted_iota(jnp.int32, (HD, 2 * HD), 1)
        kind = col // HD
        for m in range(MEM):
            source = 64 * half + QUART * kind + (col % HD) - QUART * m
            good = (lane == source) & ((col % HD) // QUART == m)
            hot = good.astype(F32).astype(BF)
            total += jnp.dot(kv_ref[m].reshape(NLIST * 16, HD), hot, preferred_element_type=F32)
        total = total.astype(BF).reshape(NLIST, 16, 2 * HD)
        key[:, 16 * half : 16 * half + 16, :] = total[:, :, :HD]
        value[:, 16 * half : 16 * half + 16, :] = total[:, :, HD:]
    keys = key[...].reshape(TOK, HD)
    values = value[...].reshape(TOK, HD)
    stat[...] = got_ref[:, STAT : STAT + SPAN, :].reshape(TOK, HD).astype(F32)
    key_sum = jnp.zeros((HD, TOK), F32)
    value_sum = jnp.zeros((HD, TOK), F32)
    for h in range(HEADS):
        q = got_ref[:, SPAN * h : SPAN * h + SPAN, :].reshape(TOK, HD)
        g = got_ref[:, QROWS + SPAN * h : QROWS + SPAN * h + SPAN, :].reshape(TOK, HD)
        norm = stat[:, h : h + 1] + stat[:, 4 + h : 5 + h]
        delta = stat[:, 8 + h : 9 + h] + stat[:, 12 + h : 13 + h]
        scores = lax.dot_general(q, keys, (((1,), (1,)), ((), ())), preferred_element_type=F32)
        probs = jnp.exp2(scores * (SCALE * LOG2E) - norm * LOG2E + bias_ref[...])
        dprobs = lax.dot_general(g, values, (((1,), (1,)), ((), ())), preferred_element_type=F32)
        dscores = (probs * (dprobs - delta)).astype(BF)
        value_sum += lax.dot_general(g, probs.astype(BF), (((0,), (0,)), ((), ())), preferred_element_type=F32)
        key_sum += lax.dot_general(q, dscores, (((0,), (0,)), ((), ())), preferred_element_type=F32)
        dq = jnp.dot(dscores, keys, preferred_element_type=F32) * SCALE
        dq_ref[:, SPAN * h : SPAN * h + SPAN, :] = dq.astype(BF).reshape(SEQ, SPAN, HD)
    key_sum = key_sum * SCALE
    for m in range(MEM):
        dkv_ref[m, 0:QUART, :] = key_sum[QUART * m : QUART * m + QUART].astype(BF)
        dkv_ref[m, QUART : 2 * QUART, :] = value_sum[QUART * m : QUART * m + QUART].astype(BF)


def attend(got, kv, bias):
    return pl.pallas_call(
        attend_kernel,
        out_shape=(
            jax.ShapeDtypeStruct((SEQ, QROWS, HD), BF),
            jax.ShapeDtypeStruct((MEM, 2 * QUART, TOK), BF),
        ),
        in_specs=[vmem(), vmem(), vmem()],
        out_specs=(vmem(), vmem()),
        scratch_shapes=[
            pltpu.VMEM((NLIST, KVCH, HD), BF),
            pltpu.VMEM((NLIST, KVCH, HD), BF),
            pltpu.VMEM((TOK, HD), F32),
        ],
        name="attend",
    )(got, kv, bias)


def spread_kernel(homes, part_ref, dq_ref, out_ref):
    out_ref[:, 0:QROWS, :] = dq_ref[...]
    total = (part_ref[0].astype(F32) + part_ref[1].astype(F32)) + (
        part_ref[2].astype(F32) + part_ref[3].astype(F32)
    )
    lane = lax.broadcasted_iota(jnp.int32, (16, HD), 1) // KVCH
    for i in range(NLIST):
        tile, place = divmod(i, 4)
        block = jnp.zeros((16, HD), F32)
        for b in range(4):
            piece = total[16 * b : 16 * b + 16, HD * tile : HD * tile + HD]
            shift = (KVCH * (b - place)) % HD
            if shift:
                piece = pltpu.roll(piece, shift, 1)
            block = jnp.where(lane == b, piece, block)
        out_ref[homes[i], pl.ds(QROWS, 16), :] = block.astype(BF)


def spread(homes, part, dq):
    return pl.pallas_call(
        spread_kernel,
        out_shape=jax.ShapeDtypeStruct((SEQ, OUT_ROWS, HD), BF),
        in_specs=[smem(), vmem(), vmem()],
        out_specs=vmem(),
        name="spread",
    )(homes, part, dq)


def settle_kernel(dest, sub, got_ref, dq_ref, dk_ref, dv_ref, acc):
    acc[...] = jnp.zeros_like(acc)
    for j in range(SEQ):
        slot = dest[j]
        for h in range(HEADS):
            dq_ref[j, :, HD * h : HD * h + HD] = got_ref[slot, pl.ds(SPAN * h, SPAN), :]

    def add(n, carry):
        spot = sub[n]

        @pl.when(spot >= 0)
        def _():
            acc[spot] += got_ref[n, pl.ds(QROWS, 16), :].astype(F32)

        return carry

    lax.fori_loop(0, SEQ, add, 0)
    lane = lax.broadcasted_iota(jnp.int32, (16, HD), 1) // KVCH
    for ref, first in ((dk_ref, 0), (dv_ref, 2)):
        for b in range(2):
            for tile in range(4):
                block = jnp.zeros((16, HD), F32)
                for place in range(4):
                    piece = acc[4 * tile + place]
                    shift = (KVCH * (place - first - b)) % HD
                    if shift:
                        piece = pltpu.roll(piece, shift, 1)
                    block = jnp.where(lane == place, piece, block)
                ref[16 * b : 16 * b + 16, HD * tile : HD * tile + HD] = block


def settle(dest, sub, got):
    return pl.pallas_call(
        settle_kernel,
        out_shape=(
            jax.ShapeDtypeStruct((SEQ, SPAN, HEADS * HD), BF),
            jax.ShapeDtypeStruct((QUART, TOK), F32),
            jax.ShapeDtypeStruct((QUART, TOK), F32),
        ),
        in_specs=[smem(), smem(), vmem()],
        out_specs=(vmem(), vmem(), vmem()),
        scratch_shapes=[pltpu.VMEM((NLIST, 16, HD), F32)],
        name="settle",
    )(dest, sub, got)


def exchanged(value, axis):
    return lax.all_to_all(value, axis, split_axis=0, concat_axis=0, tiled=True)


def local(query_rows, key_rows, value_rows, output_grad, log_norm, row_delta, dispatch, listed_spans, range_start):
    home = lax.axis_index("seq")
    kv_head = lax.axis_index("kvh")
    member = lax.axis_index("mem")
    place = jnp.stack([kv_head, member]).astype(jnp.int32)
    dest = lax.dynamic_index_in_dim(dispatch, home, 0, keepdims=False)
    at_home = listed_spans // NLIST == home
    sub = jnp.sum(jnp.where(at_home, listed_spans % NLIST + 1, 0), axis=1) - 1
    sent = pack(dest, jnp.maximum(sub, 0), place, query_rows, output_grad, key_rows, value_rows, log_norm, row_delta)
    got = exchanged(sent, "seq")

    my_list = lax.dynamic_index_in_dim(listed_spans, home, 0, keepdims=False)
    homes = my_list // NLIST
    here = dispatch == home
    spot = jnp.arange(SEQ, dtype=jnp.int32)
    span_ids = jnp.sum(jnp.where(here, spot[:, None] * SEQ + spot[None, :], 0), axis=1)
    starts = jnp.sum(jnp.where(here, range_start, 0), axis=1)
    query_pos = (span_ids[:, None] * SPAN + jnp.arange(SPAN, dtype=jnp.int32)[None, :]).reshape(-1)
    lowest = jnp.repeat(starts, SPAN)
    key_pos = (my_list[:, None] * KVCH + jnp.arange(KVCH, dtype=jnp.int32)[None, :]).reshape(-1)
    allowed = (key_pos[None, :] <= query_pos[:, None]) & (key_pos[None, :] >= lowest[:, None])
    bias = jnp.where(allowed, 0.0, -1e30).astype(F32)

    chosen = select(homes, got)
    kv = exchanged(chosen, "mem")
    dq, dkv = attend(got, kv, bias)
    part = exchanged(dkv, "mem")
    back = exchanged(spread(homes, part, dq), "seq")
    dq_out, dk_out, dv_out = settle(dest, sub, back)
    return dq_out.reshape(TOK, HEADS * HD), dk_out, dv_out


def solution(mesh):
    seq, head = mesh.axis_names
    split = Mesh(mesh.devices.reshape(SEQ, -1, MEM), (seq, "kvh", "mem"))
    both = ("kvh", "mem")
    placed = (
        P("seq", both),
        P("seq", None),
        P("seq", None),
        P("seq", both),
        P(both, "seq"),
        P(both, "seq"),
        P(),
        P(),
        P(),
    )
    return jax.shard_map(
        local,
        mesh=split,
        in_specs=placed,
        out_specs=(P("seq", both), P(both, "seq"), P(both, "seq")),
        check_vma=False,
    )
```

```python
import math

import jax
import jax.numpy as jnp
from jax import lax
from jax.experimental import pallas as pl
from jax.experimental.pallas import tpu as pltpu
from jax.sharding import Mesh
from jax.sharding import PartitionSpec as P

HD = 128
GROUP = 16
SPAN = 8
KVCH = 32
NLIST = 16
SEQ = 64
MEM = 4
HEADS = 4
TOK = 512
QROWS = HEADS * SPAN
HALF = HEADS // 2
HROWS = HALF * SPAN
ROWS_1 = 2 * HROWS + SPAN + 16
OUT_ROWS = QROWS + 16
QUART = HD // MEM
SCALE = 1.0 / math.sqrt(HD)
LOG2E = math.log2(math.e)
BF = jnp.bfloat16
PARAMS = pltpu.CompilerParams(vmem_limit_bytes=16 * 2**20)
F32 = jnp.float32


def lane_select(member):
    depth = lax.broadcasted_iota(jnp.int32, (HD, HD), 0)
    lane = lax.broadcasted_iota(jnp.int32, (HD, HD), 1) % 64
    key_hot = (depth == QUART * member + lane) & (lane < QUART)
    value_hot = (depth == QUART * member + lane - QUART) & (lane >= QUART)
    return key_hot.astype(F32).astype(BF), value_hot.astype(F32).astype(BF)


def first_kernel(
    dispatch_hbm, listed_hbm, norm_hbm, delta_hbm, q_hbm, g_hbm, k_hbm, v_hbm, out_ref,
    dispatch_ref, listed_ref, norm_ref, delta_ref, q_ref, g_ref, k_ref, v_ref,
    meta, where, stat, rows, kv, sems,
):
    home = lax.axis_index("seq")
    lanes = pl.ds(pl.multiple_of(lax.axis_index("kvh") * HD, HD), HD)
    half = pl.ds(0, HALF * HD)
    copies = [
        pltpu.make_async_copy(source, target, sems.at[index])
        for index, (source, target) in enumerate(
            (
                (dispatch_hbm, dispatch_ref),
                (listed_hbm, listed_ref),
                (norm_hbm, norm_ref),
                (delta_hbm, delta_ref),
                (k_hbm.at[:, lanes], k_ref),
                (v_hbm.at[:, lanes], v_ref),
                (q_hbm.at[:, :, half], q_ref),
                (g_hbm.at[:, :, half], g_ref),
            )
        )
    ]
    for copy in copies:
        copy.start()
    copies[0].wait()
    copies[1].wait()
    row = lax.broadcasted_iota(jnp.int32, (SEQ, SEQ), 0)
    listed = listed_ref[...]
    meta[0:1, 0:SEQ] = jnp.sum(jnp.where(row == home, dispatch_ref[...], 0), axis=0, keepdims=True)
    meta[1:2, 0:SEQ] = jnp.sum(jnp.where(listed // NLIST == home, listed % NLIST, 0), axis=0, keepdims=True)
    move = pltpu.make_async_copy(meta, where, sems.at[8])
    move.start()
    copies[2].wait()
    copies[3].wait()
    stat[...] = jnp.zeros_like(stat)
    for index, ref in enumerate((norm_ref, delta_ref)):
        value = ref[...]
        top = value.astype(BF).astype(F32)
        stat[8 * index : 8 * index + 4, :] = top
        stat[8 * index + 4 : 8 * index + 8, :] = value - top
    rows[...] = stat[...].T.astype(BF).reshape(SEQ, SPAN, HD)
    key_hot, value_hot = lane_select(lax.axis_index("mem"))
    copies[4].wait()
    copies[5].wait()
    both = jnp.dot(k_ref[...], key_hot, preferred_element_type=F32) + jnp.dot(
        v_ref[...], value_hot, preferred_element_type=F32
    )
    both = both.reshape(NLIST, 2, 16, HD)
    lane = lax.broadcasted_iota(jnp.int32, (NLIST, 16, HD), 2)
    kv[...] = jnp.where(lane < 64, both[:, 0], both[:, 1]).astype(BF)
    copies[6].wait()
    copies[7].wait()
    move.wait()
    for j in range(SEQ):
        slot = where[0, j]
        for h in range(HALF):
            out_ref[slot, pl.ds(SPAN * h, SPAN), :] = q_ref[j, :, HD * h : HD * h + HD]
            out_ref[slot, pl.ds(HROWS + SPAN * h, SPAN), :] = g_ref[j, :, HD * h : HD * h + HD]
        out_ref[slot, pl.ds(2 * HROWS, SPAN), :] = rows[j]
        out_ref[j, pl.ds(2 * HROWS + SPAN, 16), :] = kv[where[1, j]]


def vmem():
    return pl.BlockSpec(memory_space=pltpu.VMEM)


def smem():
    return pl.BlockSpec(memory_space=pltpu.SMEM)


def far():
    return pl.BlockSpec(memory_space=pltpu.HBM)


def first(dispatch, listed, norm, delta, q, g, k, v):
    return pl.pallas_call(
        first_kernel,
        out_shape=jax.ShapeDtypeStruct((SEQ, ROWS_1, HD), BF),
        in_specs=[far()] * 8,
        out_specs=vmem(),
        scratch_shapes=[
            pltpu.VMEM((SEQ, SEQ), jnp.int32),
            pltpu.VMEM((NLIST, SEQ), jnp.int32),
            pltpu.VMEM((HEADS, TOK), F32),
            pltpu.VMEM((HEADS, TOK), F32),
            pltpu.VMEM((SEQ, SPAN, HALF * HD), BF),
            pltpu.VMEM((SEQ, SPAN, HALF * HD), BF),
            pltpu.VMEM((TOK, HD), BF),
            pltpu.VMEM((TOK, HD), BF),
            pltpu.VMEM((8, HD), jnp.int32),
            pltpu.SMEM((8, HD), jnp.int32),
            pltpu.VMEM((HD, TOK), F32),
            pltpu.VMEM((SEQ, SPAN, HD), BF),
            pltpu.VMEM((NLIST, 16, HD), BF),
            pltpu.SemaphoreType.DMA((9,)),
        ],
        name="first",
    )(dispatch, listed.T, norm, delta, q, g, k, v)


def second_kernel(dest, q_ref, g_ref, out_ref):
    for j in range(SEQ):
        slot = dest[j]
        for h in range(HALF):
            out_ref[slot, pl.ds(SPAN * h, SPAN), :] = q_ref[j, :, HD * h : HD * h + HD]
            out_ref[slot, pl.ds(HROWS + SPAN * h, SPAN), :] = g_ref[j, :, HD * h : HD * h + HD]


def second(dest, q, g):
    half = pl.BlockSpec((SEQ, SPAN, HALF * HD), lambda i, d: (0, 0, 1))
    return pl.pallas_call(
        second_kernel,
        out_shape=jax.ShapeDtypeStruct((SEQ, 2 * HROWS, HD), BF),
        grid_spec=pltpu.PrefetchScalarGridSpec(
            num_scalar_prefetch=1,
            grid=(1,),
            in_specs=[half, half],
            out_specs=pl.BlockSpec((SEQ, 2 * HROWS, HD), lambda i, d: (0, 0, 0)),
        ),
        compiler_params=PARAMS,
        name="second",
    )(dest, q, g)


def select_kernel(homes, got_ref, out_ref):
    for i in range(NLIST):
        out_ref[i] = got_ref[homes[i], pl.ds(2 * HROWS + SPAN, 16), :]


def select(homes, got):
    return pl.pallas_call(
        select_kernel,
        out_shape=pltpu.VMEM((NLIST, 16, HD), BF),
        in_specs=[smem(), vmem()],
        out_specs=vmem(),
        compiler_params=PARAMS,
        name="select",
    )(homes, got)


def heads(q_at, g_at, stat, keys, values, bias_ref, dq_ref, base, key_sum, value_sum):
    for h in range(HALF):
        q = q_at(h)
        g = g_at(h)
        i = base + h
        norm = stat[:, i : i + 1] + stat[:, 4 + i : 5 + i]
        delta = stat[:, 8 + i : 9 + i] + stat[:, 12 + i : 13 + i]
        scores = lax.dot_general(q, keys, (((1,), (1,)), ((), ())), preferred_element_type=F32)
        probs = jnp.exp2(scores * (SCALE * LOG2E) - norm * LOG2E + bias_ref[...])
        dprobs = lax.dot_general(g, values, (((1,), (1,)), ((), ())), preferred_element_type=F32)
        dscores = (probs * (dprobs - delta)).astype(BF)
        value_sum += lax.dot_general(g, probs.astype(BF), (((0,), (0,)), ((), ())), preferred_element_type=F32)
        key_sum += lax.dot_general(q, dscores, (((0,), (0,)), ((), ())), preferred_element_type=F32)
        dq = jnp.dot(dscores, keys, preferred_element_type=F32) * SCALE
        dq_ref[:, SPAN * h : SPAN * h + SPAN, :] = dq.astype(BF).reshape(SEQ, SPAN, HD)
    return key_sum, value_sum


def taker(ref, offset):
    return lambda h: ref[:, offset + SPAN * h : offset + SPAN * h + SPAN, :].reshape(TOK, HD)


def early_kernel(
    got_ref, kv0, kv1, kv2, kv3, bias_ref, dq_ref, sums_ref, both_ref, stat_ref, key, value,
):
    member = lax.axis_index("mem")
    lane = lax.broadcasted_iota(jnp.int32, (HD, 2 * HD), 0)
    col = lax.broadcasted_iota(jnp.int32, (HD, 2 * HD), 1)
    for half in range(2):
        total = jnp.zeros((NLIST * 16, 2 * HD), F32)
        for s, ref in enumerate((kv0, kv1, kv2, kv3)):
            owner = lax.rem(member + (MEM - s), MEM)
            source = 64 * half + QUART * (col // HD) + (col % HD) - QUART * owner
            good = (lane == source) & ((col % HD) // QUART == owner)
            hot = good.astype(F32).astype(BF)
            total += jnp.dot(ref[...].reshape(NLIST * 16, HD), hot, preferred_element_type=F32)
        total = total.astype(BF).reshape(NLIST, 16, 2 * HD)
        key[:, 16 * half : 16 * half + 16, :] = total[:, :, :HD]
        value[:, 16 * half : 16 * half + 16, :] = total[:, :, HD:]
    keys = key[...].reshape(TOK, HD)
    values = value[...].reshape(TOK, HD)
    both_ref[0] = keys
    both_ref[1] = values
    stat = got_ref[:, 2 * HROWS : 2 * HROWS + SPAN, :].reshape(TOK, HD).astype(F32)
    stat_ref[...] = stat
    zero = jnp.zeros((HD, TOK), F32)
    key_sum, value_sum = heads(
        taker(got_ref, 0), taker(got_ref, HROWS), stat_ref, keys, values, bias_ref, dq_ref, 0, zero, zero
    )
    sums_ref[0] = key_sum
    sums_ref[1] = value_sum


def early(got, kvs, bias):
    return pl.pallas_call(
        early_kernel,
        out_shape=(
            pltpu.VMEM((SEQ, HROWS, HD), BF),
            pltpu.VMEM((2, HD, TOK), F32),
            pltpu.VMEM((2, TOK, HD), BF),
            pltpu.VMEM((TOK, HD), F32),
        ),
        in_specs=[vmem()] * 6,
        out_specs=(vmem(),) * 4,
        scratch_shapes=[pltpu.VMEM((NLIST, KVCH, HD), BF), pltpu.VMEM((NLIST, KVCH, HD), BF)],
        compiler_params=PARAMS,
        name="early",
    )(got, *kvs, bias)


def late_kernel(got_ref, sums_ref, both_ref, stat_ref, bias_ref, dq_ref, dkv_ref):
    key_sum, value_sum = heads(
        taker(got_ref, 0), taker(got_ref, HROWS), stat_ref, both_ref[0], both_ref[1], bias_ref, dq_ref, HALF,
        sums_ref[0], sums_ref[1],
    )
    key_sum = key_sum * SCALE
    for m in range(MEM):
        dkv_ref[m, 0:QUART, :] = key_sum[QUART * m : QUART * m + QUART].astype(BF)
        dkv_ref[m, QUART : 2 * QUART, :] = value_sum[QUART * m : QUART * m + QUART].astype(BF)


def late(got, sums, both, stat, bias):
    return pl.pallas_call(
        late_kernel,
        out_shape=(
            pltpu.VMEM((SEQ, HROWS, HD), BF),
            jax.ShapeDtypeStruct((MEM, 2 * QUART, TOK), BF),
        ),
        in_specs=[vmem()] * 5,
        out_specs=(vmem(), vmem()),
        compiler_params=PARAMS,
        name="late",
    )(got, sums, both, stat, bias)


def spread_kernel(homes, part_ref, early_ref, late_ref, out_ref):
    out_ref[:, 0:HROWS, :] = early_ref[...]
    out_ref[:, HROWS:QROWS, :] = late_ref[...]
    total = (part_ref[0].astype(F32) + part_ref[1].astype(F32)) + (
        part_ref[2].astype(F32) + part_ref[3].astype(F32)
    )
    lane = lax.broadcasted_iota(jnp.int32, (16, HD), 1) // KVCH
    for i in range(NLIST):
        tile, place = divmod(i, 4)
        block = jnp.zeros((16, HD), F32)
        for b in range(4):
            piece = total[16 * b : 16 * b + 16, HD * tile : HD * tile + HD]
            shift = (KVCH * (b - place)) % HD
            if shift:
                piece = pltpu.roll(piece, shift, 1)
            block = jnp.where(lane == b, piece, block)
        out_ref[homes[i], pl.ds(QROWS, 16), :] = block.astype(BF)


def spread(homes, part, dq_early, dq_late):
    return pl.pallas_call(
        spread_kernel,
        out_shape=jax.ShapeDtypeStruct((SEQ, OUT_ROWS, HD), BF),
        in_specs=[smem(), vmem(), vmem(), vmem()],
        out_specs=vmem(),
        compiler_params=PARAMS,
        name="spread",
    )(homes, part, dq_early, dq_late)


def settle_kernel(dest, sub, got_ref, dq_ref, dk_ref, dv_ref, acc):
    acc[...] = jnp.zeros_like(acc)
    for j in range(SEQ):
        slot = dest[j]
        for h in range(HEADS):
            dq_ref[j, :, HD * h : HD * h + HD] = got_ref[slot, pl.ds(SPAN * h, SPAN), :]

    for n in range(SEQ):
        acc[sub[n]] += got_ref[n, pl.ds(QROWS, 16), :].astype(F32)
    lane = lax.broadcasted_iota(jnp.int32, (16, HD), 1) // KVCH
    for ref, first in ((dk_ref, 0), (dv_ref, 2)):
        for b in range(2):
            for tile in range(4):
                block = jnp.zeros((16, HD), F32)
                for place in range(4):
                    piece = acc[4 * tile + place]
                    shift = (KVCH * (place - first - b)) % HD
                    if shift:
                        piece = pltpu.roll(piece, shift, 1)
                    block = jnp.where(lane == place, piece, block)
                ref[16 * b : 16 * b + 16, HD * tile : HD * tile + HD] = block


def settle(dest, sub, got):
    return pl.pallas_call(
        settle_kernel,
        out_shape=(
            jax.ShapeDtypeStruct((SEQ, SPAN, HEADS * HD), BF),
            jax.ShapeDtypeStruct((QUART, TOK), F32),
            jax.ShapeDtypeStruct((QUART, TOK), F32),
        ),
        in_specs=[smem(), smem(), vmem()],
        out_specs=(vmem(), vmem(), vmem()),
        scratch_shapes=[pltpu.VMEM((NLIST + 1, 16, HD), F32)],
        compiler_params=PARAMS,
        name="settle",
    )(dest, sub, got)


def near(value):
    return pltpu.with_memory_space_constraint(value, pltpu.VMEM)


def exchanged(value, axis):
    return near(lax.all_to_all(value, axis, split_axis=0, concat_axis=0, tiled=True))


def local(query_rows, key_rows, value_rows, output_grad, log_norm, row_delta, dispatch, listed_spans, range_start):
    home = lax.axis_index("seq")
    q = query_rows.reshape(SEQ, SPAN, HEADS * HD)
    g = output_grad.reshape(SEQ, SPAN, HEADS * HD)
    got_1 = exchanged(
        first(dispatch, listed_spans, log_norm, row_delta, q, g, key_rows, value_rows), "seq"
    )

    dest = lax.dynamic_index_in_dim(dispatch, home, 0, keepdims=False)
    at_home = listed_spans // NLIST == home
    sub = jnp.sum(jnp.where(at_home, listed_spans % NLIST - NLIST, 0), axis=1) + NLIST
    got_2 = exchanged(second(dest, q, g), "seq")
    my_list = lax.dynamic_index_in_dim(listed_spans, home, 0, keepdims=False)
    homes = my_list // NLIST
    here = dispatch == home
    spot = jnp.arange(SEQ, dtype=jnp.int32)
    span_ids = jnp.sum(jnp.where(here, spot[:, None] * SEQ + spot[None, :], 0), axis=1)
    starts = jnp.sum(jnp.where(here, range_start, 0), axis=1)
    query_pos = (span_ids[:, None] * SPAN + jnp.arange(SPAN, dtype=jnp.int32)[None, :]).reshape(-1)
    lowest = jnp.repeat(starts, SPAN)
    key_pos = (my_list[:, None] * KVCH + jnp.arange(KVCH, dtype=jnp.int32)[None, :]).reshape(-1)
    allowed = (key_pos[None, :] <= query_pos[:, None]) & (key_pos[None, :] >= lowest[:, None])
    bias = jnp.where(allowed, 0.0, -1e30).astype(F32)

    chosen = near(select(homes, got_1))
    kvs = [chosen] + [
        near(lax.ppermute(chosen, "mem", [(i, (i + s) % MEM) for i in range(MEM)])) for s in range(1, MEM)
    ]
    bias = near(bias)
    dq_early, sums, both, stat = map(near, early(got_1, kvs, bias))
    dq_late, dkv = late(got_2, sums, both, stat, bias)
    part = exchanged(dkv, "mem")
    back = exchanged(spread(homes, part, dq_early, near(dq_late)), "seq")
    dq_out, dk_out, dv_out = settle(dest, sub, back)
    return dq_out.reshape(TOK, HEADS * HD), dk_out, dv_out


def solution(mesh):
    seq, head = mesh.axis_names
    split = Mesh(mesh.devices.reshape(SEQ, -1, MEM), (seq, "kvh", "mem"))
    both = ("kvh", "mem")
    placed = (
        P("seq", both),
        P("seq", None),
        P("seq", None),
        P("seq", both),
        P(both, "seq"),
        P(both, "seq"),
        P(),
        P(),
        P(),
    )
    return jax.shard_map(
        local,
        mesh=split,
        in_specs=placed,
        out_specs=(P("seq", both), P(both, "seq"), P(both, "seq")),
        check_vma=False,
    )
```

```python
import math

import jax
import jax.numpy as jnp
from jax import lax
from jax.experimental import pallas as pl
from jax.experimental.pallas import tpu as pltpu
from jax.sharding import Mesh
from jax.sharding import PartitionSpec as P

HD = 128
GROUP = 16
SPAN = 8
KVCH = 32
NLIST = 16
SEQ = 64
MEM = 4
HEADS = 4
TOK = 512
QROWS = HEADS * SPAN
HALF = HEADS
HROWS = HALF * SPAN
ROWS_1 = 2 * HROWS + SPAN + 16
OUT_ROWS = QROWS + 16
QUART = HD // MEM
SCALE = 1.0 / math.sqrt(HD)
LOG2E = math.log2(math.e)
BF = jnp.bfloat16
PARAMS = pltpu.CompilerParams(vmem_limit_bytes=16 * 2**20)
F32 = jnp.float32


def lane_select(member):
    depth = lax.broadcasted_iota(jnp.int32, (HD, HD), 0)
    lane = lax.broadcasted_iota(jnp.int32, (HD, HD), 1) % 64
    key_hot = (depth == QUART * member + lane) & (lane < QUART)
    value_hot = (depth == QUART * member + lane - QUART) & (lane >= QUART)
    return key_hot.astype(F32).astype(BF), value_hot.astype(F32).astype(BF)


def first_kernel(
    dispatch_hbm, listed_hbm, norm_hbm, delta_hbm, q_hbm, g_hbm, k_hbm, v_hbm, out_ref,
    dispatch_ref, listed_ref, norm_ref, delta_ref, q_ref, g_ref, k_ref, v_ref,
    meta, where, stat, rows, kv, sems,
):
    home = lax.axis_index("seq")
    lanes = pl.ds(pl.multiple_of(lax.axis_index("kvh") * HD, HD), HD)
    half = pl.ds(0, HALF * HD)
    copies = [
        pltpu.make_async_copy(source, target, sems.at[index])
        for index, (source, target) in enumerate(
            (
                (dispatch_hbm, dispatch_ref),
                (listed_hbm, listed_ref),
                (norm_hbm, norm_ref),
                (delta_hbm, delta_ref),
                (k_hbm.at[:, lanes], k_ref),
                (v_hbm.at[:, lanes], v_ref),
                (q_hbm.at[:, :, half], q_ref),
                (g_hbm.at[:, :, half], g_ref),
            )
        )
    ]
    for copy in copies:
        copy.start()
    copies[0].wait()
    copies[1].wait()
    row = lax.broadcasted_iota(jnp.int32, (SEQ, SEQ), 0)
    listed = listed_ref[...]
    meta[0:1, 0:SEQ] = jnp.sum(jnp.where(row == home, dispatch_ref[...], 0), axis=0, keepdims=True)
    meta[1:2, 0:SEQ] = jnp.sum(jnp.where(listed // NLIST == home, listed % NLIST, 0), axis=0, keepdims=True)
    move = pltpu.make_async_copy(meta, where, sems.at[8])
    move.start()
    copies[2].wait()
    copies[3].wait()
    stat[...] = jnp.zeros_like(stat)
    for index, ref in enumerate((norm_ref, delta_ref)):
        value = ref[...]
        top = value.astype(BF).astype(F32)
        stat[8 * index : 8 * index + 4, :] = top
        stat[8 * index + 4 : 8 * index + 8, :] = value - top
    rows[...] = stat[...].T.astype(BF).reshape(SEQ, SPAN, HD)
    key_hot, value_hot = lane_select(lax.axis_index("mem"))
    copies[4].wait()
    copies[5].wait()
    both = jnp.dot(k_ref[...], key_hot, preferred_element_type=F32) + jnp.dot(
        v_ref[...], value_hot, preferred_element_type=F32
    )
    both = both.reshape(NLIST, 2, 16, HD)
    lane = lax.broadcasted_iota(jnp.int32, (NLIST, 16, HD), 2)
    kv[...] = jnp.where(lane < 64, both[:, 0], both[:, 1]).astype(BF)
    copies[6].wait()
    copies[7].wait()
    move.wait()
    for j in range(SEQ):
        slot = where[0, j]
        for h in range(HALF):
            out_ref[slot, pl.ds(SPAN * h, SPAN), :] = q_ref[j, :, HD * h : HD * h + HD]
            out_ref[slot, pl.ds(HROWS + SPAN * h, SPAN), :] = g_ref[j, :, HD * h : HD * h + HD]
        out_ref[slot, pl.ds(2 * HROWS, SPAN), :] = rows[j]
        out_ref[j, pl.ds(2 * HROWS + SPAN, 16), :] = kv[where[1, j]]


def vmem():
    return pl.BlockSpec(memory_space=pltpu.VMEM)


def smem():
    return pl.BlockSpec(memory_space=pltpu.SMEM)


def far():
    return pl.BlockSpec(memory_space=pltpu.HBM)


def first(dispatch, listed, norm, delta, q, g, k, v):
    return pl.pallas_call(
        first_kernel,
        out_shape=jax.ShapeDtypeStruct((SEQ, ROWS_1, HD), BF),
        in_specs=[far()] * 8,
        out_specs=vmem(),
        scratch_shapes=[
            pltpu.VMEM((SEQ, SEQ), jnp.int32),
            pltpu.VMEM((NLIST, SEQ), jnp.int32),
            pltpu.VMEM((HEADS, TOK), F32),
            pltpu.VMEM((HEADS, TOK), F32),
            pltpu.VMEM((SEQ, SPAN, HALF * HD), BF),
            pltpu.VMEM((SEQ, SPAN, HALF * HD), BF),
            pltpu.VMEM((TOK, HD), BF),
            pltpu.VMEM((TOK, HD), BF),
            pltpu.VMEM((8, HD), jnp.int32),
            pltpu.SMEM((8, HD), jnp.int32),
            pltpu.VMEM((HD, TOK), F32),
            pltpu.VMEM((SEQ, SPAN, HD), BF),
            pltpu.VMEM((NLIST, 16, HD), BF),
            pltpu.SemaphoreType.DMA((9,)),
        ],
        name="first",
    )(dispatch, listed.T, norm, delta, q, g, k, v)


def select_kernel(homes, got_ref, out_ref):
    for i in range(NLIST):
        block = got_ref[homes[i], pl.ds(2 * HROWS + SPAN, 16), :]
        for m in range(MEM):
            out_ref[m, i] = block


def select(homes, got):
    return pl.pallas_call(
        select_kernel,
        out_shape=jax.ShapeDtypeStruct((MEM, NLIST, 16, HD), BF),
        in_specs=[smem(), vmem()],
        out_specs=vmem(),
        compiler_params=PARAMS,
        name="select",
    )(homes, got)


def heads(q_at, g_at, stat, keys, values, bias_ref, dq_ref, base, key_sum, value_sum):
    for h in range(HALF):
        q = q_at(h)
        g = g_at(h)
        i = base + h
        norm = stat[:, i : i + 1] + stat[:, 4 + i : 5 + i]
        delta = stat[:, 8 + i : 9 + i] + stat[:, 12 + i : 13 + i]
        scores = lax.dot_general(q, keys, (((1,), (1,)), ((), ())), preferred_element_type=F32)
        probs = jnp.exp2(scores * (SCALE * LOG2E) - norm * LOG2E + bias_ref[...].astype(F32))
        dprobs = lax.dot_general(g, values, (((1,), (1,)), ((), ())), preferred_element_type=F32)
        dscores = (probs * (dprobs - delta)).astype(BF)
        value_sum += lax.dot_general(g, probs.astype(BF), (((0,), (0,)), ((), ())), preferred_element_type=F32)
        key_sum += lax.dot_general(q, dscores, (((0,), (0,)), ((), ())), preferred_element_type=F32)
        dq = jnp.dot(dscores, keys, preferred_element_type=F32) * SCALE
        dq_ref[:, SPAN * h : SPAN * h + SPAN, :] = dq.astype(BF).reshape(SEQ, SPAN, HD)
    return key_sum, value_sum


def taker(ref, offset):
    return lambda h: ref[:, offset + SPAN * h : offset + SPAN * h + SPAN, :].reshape(TOK, HD)


def attend_kernel(got_ref, kv_ref, bias_ref, dq_ref, dkv_ref, key, value, stat_ref):
    lane = lax.broadcasted_iota(jnp.int32, (HD, 2 * HD), 0)
    col = lax.broadcasted_iota(jnp.int32, (HD, 2 * HD), 1)
    for half in range(2):
        total = jnp.zeros((NLIST * 16, 2 * HD), F32)
        for m in range(MEM):
            source = 64 * half + QUART * (col // HD) + (col % HD) - QUART * m
            good = (lane == source) & ((col % HD) // QUART == m)
            hot = good.astype(F32).astype(BF)
            total += jnp.dot(kv_ref[m].reshape(NLIST * 16, HD), hot, preferred_element_type=F32)
        total = total.astype(BF).reshape(NLIST, 16, 2 * HD)
        key[:, 16 * half : 16 * half + 16, :] = total[:, :, :HD]
        value[:, 16 * half : 16 * half + 16, :] = total[:, :, HD:]
    keys = key[...].reshape(TOK, HD)
    values = value[...].reshape(TOK, HD)
    stat_ref[...] = got_ref[:, 2 * HROWS : 2 * HROWS + SPAN, :].reshape(TOK, HD).astype(F32)
    zero = jnp.zeros((HD, TOK), F32)
    key_sum, value_sum = heads(
        taker(got_ref, 0), taker(got_ref, HROWS), stat_ref, keys, values, bias_ref, dq_ref, 0, zero, zero
    )
    key_sum = key_sum * SCALE
    for m in range(MEM):
        dkv_ref[m, 0:QUART, :] = key_sum[QUART * m : QUART * m + QUART].astype(BF)
        dkv_ref[m, QUART : 2 * QUART, :] = value_sum[QUART * m : QUART * m + QUART].astype(BF)


def attend(got, kv, bias):
    return pl.pallas_call(
        attend_kernel,
        out_shape=(
            pltpu.VMEM((SEQ, QROWS, HD), BF),
            jax.ShapeDtypeStruct((MEM, 2 * QUART, TOK), BF),
        ),
        in_specs=[vmem()] * 3,
        out_specs=(vmem(),) * 2,
        scratch_shapes=[
            pltpu.VMEM((NLIST, KVCH, HD), BF),
            pltpu.VMEM((NLIST, KVCH, HD), BF),
            pltpu.VMEM((TOK, HD), F32),
        ],
        compiler_params=PARAMS,
        name="attend",
    )(got, kv, bias)


def spread_kernel(homes, part_ref, dq_ref, out_ref):
    out_ref[:, 0:QROWS, :] = dq_ref[...]
    total = (part_ref[0].astype(F32) + part_ref[1].astype(F32)) + (
        part_ref[2].astype(F32) + part_ref[3].astype(F32)
    )
    lane = lax.broadcasted_iota(jnp.int32, (16, HD), 1) // KVCH
    for i in range(NLIST):
        tile, place = divmod(i, 4)
        block = jnp.zeros((16, HD), F32)
        for b in range(4):
            piece = total[16 * b : 16 * b + 16, HD * tile : HD * tile + HD]
            shift = (KVCH * (b - place)) % HD
            if shift:
                piece = pltpu.roll(piece, shift, 1)
            block = jnp.where(lane == b, piece, block)
        out_ref[homes[i], pl.ds(QROWS, 16), :] = block.astype(BF)


def spread(homes, part, dq):
    return pl.pallas_call(
        spread_kernel,
        out_shape=jax.ShapeDtypeStruct((SEQ, OUT_ROWS, HD), BF),
        in_specs=[smem(), vmem(), vmem()],
        out_specs=vmem(),
        compiler_params=PARAMS,
        name="spread",
    )(homes, part, dq)


def settle_kernel(dest, sub, got_ref, dq_ref, dk_ref, dv_ref, acc):
    acc[...] = jnp.zeros_like(acc)
    for j in range(SEQ):
        slot = dest[j]
        for h in range(HEADS):
            dq_ref[j, :, HD * h : HD * h + HD] = got_ref[slot, pl.ds(SPAN * h, SPAN), :]

    for n in range(SEQ):
        acc[sub[n]] += got_ref[n, pl.ds(QROWS, 16), :].astype(F32)
    lane = lax.broadcasted_iota(jnp.int32, (16, HD), 1) // KVCH
    for ref, first in ((dk_ref, 0), (dv_ref, 2)):
        for b in range(2):
            for tile in range(4):
                block = jnp.zeros((16, HD), F32)
                for place in range(4):
                    piece = acc[4 * tile + place]
                    shift = (KVCH * (place - first - b)) % HD
                    if shift:
                        piece = pltpu.roll(piece, shift, 1)
                    block = jnp.where(lane == place, piece, block)
                ref[16 * b : 16 * b + 16, HD * tile : HD * tile + HD] = block


def settle(dest, sub, got):
    return pl.pallas_call(
        settle_kernel,
        out_shape=(
            jax.ShapeDtypeStruct((SEQ, SPAN, HEADS * HD), BF),
            jax.ShapeDtypeStruct((QUART, TOK), F32),
            jax.ShapeDtypeStruct((QUART, TOK), F32),
        ),
        in_specs=[smem(), smem(), vmem()],
        out_specs=(vmem(), vmem(), vmem()),
        scratch_shapes=[pltpu.VMEM((NLIST + 1, 16, HD), F32)],
        compiler_params=PARAMS,
        name="settle",
    )(dest, sub, got)


def near(value):
    return pltpu.with_memory_space_constraint(value, pltpu.VMEM)


def exchanged(value, axis):
    return near(lax.all_to_all(value, axis, split_axis=0, concat_axis=0, tiled=True))


def local(query_rows, key_rows, value_rows, output_grad, log_norm, row_delta, dispatch, listed_spans, range_start):
    home = lax.axis_index("seq")
    q = query_rows.reshape(SEQ, SPAN, HEADS * HD)
    g = output_grad.reshape(SEQ, SPAN, HEADS * HD)
    got_1 = exchanged(
        first(dispatch, listed_spans, log_norm, row_delta, q, g, key_rows, value_rows), "seq"
    )

    dest = lax.dynamic_index_in_dim(dispatch, home, 0, keepdims=False)
    at_home = listed_spans // NLIST == home
    sub = jnp.sum(jnp.where(at_home, listed_spans % NLIST - NLIST, 0), axis=1) + NLIST
    my_list = lax.dynamic_index_in_dim(listed_spans, home, 0, keepdims=False)
    homes = my_list // NLIST
    here = dispatch == home
    spot = jnp.arange(SEQ, dtype=jnp.int32)
    span_ids = jnp.sum(jnp.where(here, spot[:, None] * SEQ + spot[None, :], 0), axis=1)
    starts = jnp.sum(jnp.where(here, range_start, 0), axis=1)
    query_pos = (span_ids[:, None] * SPAN + jnp.arange(SPAN, dtype=jnp.int32)[None, :]).reshape(-1)
    lowest = jnp.repeat(starts, SPAN)
    key_pos = (my_list[:, None] * KVCH + jnp.arange(KVCH, dtype=jnp.int32)[None, :]).reshape(-1)
    allowed = (key_pos[None, :] <= query_pos[:, None]) & (key_pos[None, :] >= lowest[:, None])
    bias = jnp.where(allowed, 0.0, -1e30).astype(BF)

    chosen = select(homes, got_1)
    kv = exchanged(chosen, "mem")
    dq, dkv = attend(got_1, kv, near(bias))
    part = exchanged(dkv, "mem")
    back = exchanged(spread(homes, part, near(dq)), "seq")
    dq_out, dk_out, dv_out = settle(dest, sub, back)
    return dq_out.reshape(TOK, HEADS * HD), dk_out, dv_out


def solution(mesh):
    seq, head = mesh.axis_names
    split = Mesh(mesh.devices.reshape(SEQ, -1, MEM), (seq, "kvh", "mem"))
    both = ("kvh", "mem")
    placed = (
        P("seq", both),
        P("seq", None),
        P("seq", None),
        P("seq", both),
        P(both, "seq"),
        P(both, "seq"),
        P(),
        P(),
        P(),
    )
    return jax.shard_map(
        local,
        mesh=split,
        in_specs=placed,
        out_specs=(P("seq", both), P(both, "seq"), P(both, "seq")),
        check_vma=False,
    )
```

```python
import math

import jax
import jax.numpy as jnp
from jax import lax
from jax.experimental import pallas as pl
from jax.experimental.pallas import tpu as pltpu
from jax.sharding import Mesh
from jax.sharding import PartitionSpec as P

HD = 128
GROUP = 16
SPAN = 8
KVCH = 32
NLIST = 16
SEQ = 64
MEM = 4
HEADS = 4
TOK = 512
QROWS = HEADS * SPAN
HALF = HEADS
HROWS = HALF * SPAN
ROWS_1 = 2 * HROWS + SPAN + 16
OUT_ROWS = QROWS + 16
QUART = HD // MEM
SCALE = 1.0 / math.sqrt(HD)
LOG2E = math.log2(math.e)
BF = jnp.bfloat16
PARAMS = pltpu.CompilerParams(vmem_limit_bytes=16 * 2**20)
F32 = jnp.float32


def lane_select(member):
    depth = lax.broadcasted_iota(jnp.int32, (HD, HD), 0)
    lane = lax.broadcasted_iota(jnp.int32, (HD, HD), 1) % 64
    key_hot = (depth == QUART * member + lane) & (lane < QUART)
    value_hot = (depth == QUART * member + lane - QUART) & (lane >= QUART)
    return key_hot.astype(F32).astype(BF), value_hot.astype(F32).astype(BF)


def first_kernel(
    dispatch_hbm, listed_hbm, norm_hbm, delta_hbm, q_hbm, g_hbm, k_hbm, v_hbm, out_ref,
    dispatch_ref, listed_ref, norm_ref, delta_ref, q_ref, g_ref, k_ref, v_ref,
    meta, where, stat, rows, kv, sems,
):
    home = lax.axis_index("seq")
    lanes = pl.ds(pl.multiple_of(lax.axis_index("kvh") * HD, HD), HD)
    half = pl.ds(0, HALF * HD)
    copies = [
        pltpu.make_async_copy(source, target, sems.at[index])
        for index, (source, target) in enumerate(
            (
                (dispatch_hbm, dispatch_ref),
                (listed_hbm, listed_ref),
                (norm_hbm, norm_ref),
                (delta_hbm, delta_ref),
                (k_hbm.at[:, lanes], k_ref),
                (v_hbm.at[:, lanes], v_ref),
                (q_hbm.at[:, :, half], q_ref),
                (g_hbm.at[:, :, half], g_ref),
            )
        )
    ]
    for copy in copies:
        copy.start()
    copies[0].wait()
    copies[1].wait()
    row = lax.broadcasted_iota(jnp.int32, (SEQ, SEQ), 0)
    listed = listed_ref[...]
    meta[0:1, 0:SEQ] = jnp.sum(jnp.where(row == home, dispatch_ref[...], 0), axis=0, keepdims=True)
    meta[1:2, 0:SEQ] = jnp.sum(jnp.where(listed // NLIST == home, listed % NLIST, 0), axis=0, keepdims=True)
    move = pltpu.make_async_copy(meta, where, sems.at[8])
    move.start()
    copies[2].wait()
    copies[3].wait()
    stat[...] = jnp.zeros_like(stat)
    for index, ref in enumerate((norm_ref, delta_ref)):
        value = ref[...]
        top = value.astype(BF).astype(F32)
        stat[8 * index : 8 * index + 4, :] = top
        stat[8 * index + 4 : 8 * index + 8, :] = value - top
    rows[...] = stat[...].T.astype(BF).reshape(SEQ, SPAN, HD)
    key_hot, value_hot = lane_select(lax.axis_index("mem"))
    copies[4].wait()
    copies[5].wait()
    both = jnp.dot(k_ref[...], key_hot, preferred_element_type=F32) + jnp.dot(
        v_ref[...], value_hot, preferred_element_type=F32
    )
    both = both.reshape(NLIST, 2, 16, HD)
    lane = lax.broadcasted_iota(jnp.int32, (NLIST, 16, HD), 2)
    kv[...] = jnp.where(lane < 64, both[:, 0], both[:, 1]).astype(BF)
    copies[6].wait()
    copies[7].wait()
    move.wait()
    for j in range(SEQ):
        slot = where[0, j]
        for h in range(HALF):
            out_ref[slot, pl.ds(SPAN * h, SPAN), :] = q_ref[j, :, HD * h : HD * h + HD]
            out_ref[slot, pl.ds(HROWS + SPAN * h, SPAN), :] = g_ref[j, :, HD * h : HD * h + HD]
        out_ref[slot, pl.ds(2 * HROWS, SPAN), :] = rows[j]
        out_ref[j, pl.ds(2 * HROWS + SPAN, 16), :] = kv[where[1, j]]


def vmem():
    return pl.BlockSpec(memory_space=pltpu.VMEM)


def smem():
    return pl.BlockSpec(memory_space=pltpu.SMEM)


def far():
    return pl.BlockSpec(memory_space=pltpu.HBM)


def first(dispatch, listed, norm, delta, q, g, k, v):
    return pl.pallas_call(
        first_kernel,
        out_shape=jax.ShapeDtypeStruct((SEQ, ROWS_1, HD), BF),
        in_specs=[far()] * 8,
        out_specs=vmem(),
        scratch_shapes=[
            pltpu.VMEM((SEQ, SEQ), jnp.int32),
            pltpu.VMEM((NLIST, SEQ), jnp.int32),
            pltpu.VMEM((HEADS, TOK), F32),
            pltpu.VMEM((HEADS, TOK), F32),
            pltpu.VMEM((SEQ, SPAN, HALF * HD), BF),
            pltpu.VMEM((SEQ, SPAN, HALF * HD), BF),
            pltpu.VMEM((TOK, HD), BF),
            pltpu.VMEM((TOK, HD), BF),
            pltpu.VMEM((8, HD), jnp.int32),
            pltpu.SMEM((8, HD), jnp.int32),
            pltpu.VMEM((HD, TOK), F32),
            pltpu.VMEM((SEQ, SPAN, HD), BF),
            pltpu.VMEM((NLIST, 16, HD), BF),
            pltpu.SemaphoreType.DMA((9,)),
        ],
        name="first",
    )(dispatch, listed.T, norm, delta, q, g, k, v)


def select_kernel(homes, got_ref, out_ref):
    for i in range(NLIST):
        block = got_ref[homes[i], pl.ds(2 * HROWS + SPAN, 16), :]
        for m in range(MEM):
            out_ref[m, i] = block


def select(homes, got):
    return pl.pallas_call(
        select_kernel,
        out_shape=pltpu.VMEM((MEM, NLIST, 16, HD), BF),
        in_specs=[smem(), vmem()],
        out_specs=vmem(),
        compiler_params=PARAMS,
        name="select",
    )(homes, got)


def heads(q_at, g_at, stat, keys, values, bias_ref, dq_ref, base, key_sum, value_sum):
    for h in range(HALF):
        q = q_at(h)
        g = g_at(h)
        i = base + h
        norm = stat[:, i : i + 1] + stat[:, 4 + i : 5 + i]
        delta = stat[:, 8 + i : 9 + i] + stat[:, 12 + i : 13 + i]
        scores = lax.dot_general(q, keys, (((1,), (1,)), ((), ())), preferred_element_type=F32)
        probs = jnp.exp2(scores * (SCALE * LOG2E) - norm * LOG2E + bias_ref[...].astype(F32))
        dprobs = lax.dot_general(g, values, (((1,), (1,)), ((), ())), preferred_element_type=F32)
        dscores = (probs * (dprobs - delta)).astype(BF)
        value_sum += lax.dot_general(g, probs.astype(BF), (((0,), (0,)), ((), ())), preferred_element_type=F32)
        key_sum += lax.dot_general(q, dscores, (((0,), (0,)), ((), ())), preferred_element_type=F32)
        dq = jnp.dot(dscores, keys, preferred_element_type=F32) * SCALE
        dq_ref[:, SPAN * h : SPAN * h + SPAN, :] = dq.astype(BF).reshape(SEQ, SPAN, HD)
    return key_sum, value_sum


def taker(ref, offset):
    return lambda h: ref[:, offset + SPAN * h : offset + SPAN * h + SPAN, :].reshape(TOK, HD)


def attend_kernel(got_ref, kv_ref, bias_ref, dq_ref, dkv_ref, key, value, stat_ref):
    lane = lax.broadcasted_iota(jnp.int32, (HD, 2 * HD), 0)
    col = lax.broadcasted_iota(jnp.int32, (HD, 2 * HD), 1)
    for half in range(2):
        total = jnp.zeros((NLIST * 16, 2 * HD), F32)
        for m in range(MEM):
            source = 64 * half + QUART * (col // HD) + (col % HD) - QUART * m
            good = (lane == source) & ((col % HD) // QUART == m)
            hot = good.astype(F32).astype(BF)
            total += jnp.dot(kv_ref[m].reshape(NLIST * 16, HD), hot, preferred_element_type=F32)
        total = total.astype(BF).reshape(NLIST, 16, 2 * HD)
        key[:, 16 * half : 16 * half + 16, :] = total[:, :, :HD]
        value[:, 16 * half : 16 * half + 16, :] = total[:, :, HD:]
    keys = key[...].reshape(TOK, HD)
    values = value[...].reshape(TOK, HD)
    stat_ref[...] = got_ref[:, 2 * HROWS : 2 * HROWS + SPAN, :].reshape(TOK, HD).astype(F32)
    zero = jnp.zeros((HD, TOK), F32)
    key_sum, value_sum = heads(
        taker(got_ref, 0), taker(got_ref, HROWS), stat_ref, keys, values, bias_ref, dq_ref, 0, zero, zero
    )
    key_sum = key_sum * SCALE
    for m in range(MEM):
        dkv_ref[m, 0:QUART, :] = key_sum[QUART * m : QUART * m + QUART].astype(BF)
        dkv_ref[m, QUART : 2 * QUART, :] = value_sum[QUART * m : QUART * m + QUART].astype(BF)


def attend(got, kv, bias):
    return pl.pallas_call(
        attend_kernel,
        out_shape=(
            pltpu.VMEM((SEQ, QROWS, HD), BF),
            jax.ShapeDtypeStruct((MEM, 2 * QUART, TOK), BF),
        ),
        in_specs=[vmem()] * 3,
        out_specs=(vmem(),) * 2,
        scratch_shapes=[
            pltpu.VMEM((NLIST, KVCH, HD), BF),
            pltpu.VMEM((NLIST, KVCH, HD), BF),
            pltpu.VMEM((TOK, HD), F32),
        ],
        compiler_params=PARAMS,
        name="attend",
    )(got, kv, bias)


def spread_kernel(homes, part_ref, dq_ref, out_ref):
    out_ref[:, 0:QROWS, :] = dq_ref[...]
    total = (part_ref[0].astype(F32) + part_ref[1].astype(F32)) + (
        part_ref[2].astype(F32) + part_ref[3].astype(F32)
    )
    lane = lax.broadcasted_iota(jnp.int32, (16, HD), 1) // KVCH
    for i in range(NLIST):
        tile, place = divmod(i, 4)
        block = jnp.zeros((16, HD), F32)
        for b in range(4):
            piece = total[16 * b : 16 * b + 16, HD * tile : HD * tile + HD]
            shift = (KVCH * (b - place)) % HD
            if shift:
                piece = pltpu.roll(piece, shift, 1)
            block = jnp.where(lane == b, piece, block)
        out_ref[homes[i], pl.ds(QROWS, 16), :] = block.astype(BF)


def spread(homes, part, dq):
    return pl.pallas_call(
        spread_kernel,
        out_shape=jax.ShapeDtypeStruct((SEQ, OUT_ROWS, HD), BF),
        in_specs=[smem(), vmem(), vmem()],
        out_specs=vmem(),
        compiler_params=PARAMS,
        name="spread",
    )(homes, part, dq)


def settle_kernel(dest, sub, got_ref, dq_ref, dk_ref, dv_ref, acc, *others):
    parts = (acc, *others)
    for part in parts:
        part[...] = jnp.zeros_like(part)
    for j in range(SEQ):
        slot = dest[j]
        for h in range(HEADS):
            dq_ref[j, :, HD * h : HD * h + HD] = got_ref[slot, pl.ds(SPAN * h, SPAN), :]

    for n in range(SEQ):
        parts[n % len(parts)][sub[n]] += got_ref[n, pl.ds(QROWS, 16), :].astype(F32)
    acc[...] = (parts[0][...] + parts[1][...]) + (parts[2][...] + parts[3][...])
    lane = lax.broadcasted_iota(jnp.int32, (16, HD), 1) // KVCH
    for ref, first in ((dk_ref, 0), (dv_ref, 2)):
        for b in range(2):
            for tile in range(4):
                block = jnp.zeros((16, HD), F32)
                for place in range(4):
                    piece = acc[4 * tile + place]
                    shift = (KVCH * (place - first - b)) % HD
                    if shift:
                        piece = pltpu.roll(piece, shift, 1)
                    block = jnp.where(lane == place, piece, block)
                ref[16 * b : 16 * b + 16, HD * tile : HD * tile + HD] = block


def settle(dest, sub, got):
    return pl.pallas_call(
        settle_kernel,
        out_shape=(
            jax.ShapeDtypeStruct((SEQ, SPAN, HEADS * HD), BF),
            jax.ShapeDtypeStruct((QUART, TOK), F32),
            jax.ShapeDtypeStruct((QUART, TOK), F32),
        ),
        in_specs=[smem(), smem(), vmem()],
        out_specs=(vmem(), vmem(), vmem()),
        scratch_shapes=[pltpu.VMEM((NLIST + 1, 16, HD), F32)] * 4,
        compiler_params=PARAMS,
        name="settle",
    )(dest, sub, got)


def near(value):
    return pltpu.with_memory_space_constraint(value, pltpu.VMEM)


def exchanged(value, axis):
    return near(lax.all_to_all(value, axis, split_axis=0, concat_axis=0, tiled=True))


def local(query_rows, key_rows, value_rows, output_grad, log_norm, row_delta, dispatch, listed_spans, range_start):
    home = lax.axis_index("seq")
    q = query_rows.reshape(SEQ, SPAN, HEADS * HD)
    g = output_grad.reshape(SEQ, SPAN, HEADS * HD)
    got_1 = exchanged(
        first(dispatch, listed_spans, log_norm, row_delta, q, g, key_rows, value_rows), "seq"
    )

    dest = lax.dynamic_index_in_dim(dispatch, home, 0, keepdims=False)
    at_home = listed_spans // NLIST == home
    sub = jnp.sum(jnp.where(at_home, listed_spans % NLIST - NLIST, 0), axis=1) + NLIST
    my_list = lax.dynamic_index_in_dim(listed_spans, home, 0, keepdims=False)
    homes = my_list // NLIST
    here = dispatch == home
    spot = jnp.arange(SEQ, dtype=jnp.int32)
    span_ids = jnp.sum(jnp.where(here, spot[:, None] * SEQ + spot[None, :], 0), axis=1)
    starts = jnp.sum(jnp.where(here, range_start, 0), axis=1)
    query_pos = (span_ids[:, None] * SPAN + jnp.arange(SPAN, dtype=jnp.int32)[None, :]).reshape(-1)
    lowest = jnp.repeat(starts, SPAN)
    key_pos = (my_list[:, None] * KVCH + jnp.arange(KVCH, dtype=jnp.int32)[None, :]).reshape(-1)
    allowed = (key_pos[None, :] <= query_pos[:, None]) & (key_pos[None, :] >= lowest[:, None])
    bias = jnp.where(allowed, 0.0, -1e30).astype(BF)

    chosen = select(homes, got_1)
    kv = exchanged(chosen, "mem")
    dq, dkv = attend(got_1, kv, near(bias))
    part = exchanged(dkv, "mem")
    back = exchanged(spread(homes, part, near(dq)), "seq")
    dq_out, dk_out, dv_out = settle(dest, sub, back)
    return dq_out.reshape(TOK, HEADS * HD), dk_out, dv_out


def solution(mesh):
    seq, head = mesh.axis_names
    split = Mesh(mesh.devices.reshape(SEQ, -1, MEM), (seq, "kvh", "mem"))
    both = ("kvh", "mem")
    placed = (
        P("seq", both),
        P("seq", None),
        P("seq", None),
        P("seq", both),
        P(both, "seq"),
        P(both, "seq"),
        P(),
        P(),
        P(),
    )
    return jax.shard_map(
        local,
        mesh=split,
        in_specs=placed,
        out_specs=(P("seq", both), P(both, "seq"), P(both, "seq")),
        check_vma=False,
    )
```
